128 devices in a mesh: var: 4 (over z_hi, core), space: 32 (over z_lo, x, y).
Axes of the slice: x: 4, y: 4, z: 4 (z_hi: 2, z_lo: 2; z = z_hi * 2 + z_lo), core: 2. Of those that a mesh axis runs over, the one named last changes fastest.
Arguments:
- fields: bfloat16 [8, 1024, 131072], P('var', None, 'space'), may hold values from -6 to 6
- eigenfunctions: bfloat16 [8, 64, 131072], P('var', None, 'space'), may hold values from -0.015625 to 0.015625
- start: float32 [512, 128], replicated, may hold values from -6 to 6
- grid_count: int32 [8], replicated, may hold values from 65536 to 131072
Outputs:
- loadings: bfloat16 [8, 128, 131072], P('var', None, 'space')
- component_scores: float32 [1024, 128], replicated
- explained: float32 [8, 1024], P('var')
The draws below stay inside these ranges and needn't reach their ends.
Inputs may be any that keep to these rules, and one draw needn't show every extreme that they name: The grid of variable v is its points 0 to grid_count[v] - 1.
All inputs are finite; a program needn't handle non-finite values.
Results may differ from the reference program's by a relative error of at most 0.005.
Values sent between devices are 32-bit elements; how exact they have to be, the bound alone decides.
No kernel may reach another device: no remote copies, remote signals or barrier semaphores. Data moves between devices by JAX's collectives and lax.ppermute only.
A program may use at most 64 MiB of HBM per device.

```python
import jax
import jax.numpy as jnp
from jax import lax

V = 8
M = 64
K = 128
SWEEPS = 2
NS = 1024
G = 131072
JD = 512


def with_ends(array, rng, low, high):
    shape = array.shape
    index_at = [jax.random.randint(jax.random.fold_in(rng, axis), (), 0, shape[axis]) for axis in range(len(shape))]
    array = array.at[tuple(index_at)].set(low)
    longest = shape.index(max(shape))
    index_at[longest] = (index_at[longest] + 1) % shape[longest]
    return array.at[tuple(index_at)].set(high)


def block_scale(rng, dims, pieces, low, top_value):
    level, own = 1.0, jax.random.fold_in(rng, 6)
    for dim, blocks in pieces:
        heights = jnp.exp(jax.random.uniform(jax.random.fold_in(own, dim), (blocks,), jnp.float32, low / len(pieces), top_value / len(pieces)))
        level = level * jnp.repeat(heights, dims[dim] // blocks).reshape([-1 if axis == dim else 1 for axis in range(len(dims))])
    return level


def gaussian(stream_key, dims, scale, most, split=(), kind=jnp.bfloat16):
    level = block_scale(stream_key, dims, split, -0.22, 0.18) if split else 1.0
    array = jax.random.normal(stream_key, dims, jnp.float32) * scale * level
    return jnp.minimum(jnp.maximum(array, -most), most).astype(kind)


def setup_inputs(seed: int = 0) -> dict:
    keys = jax.random.split(jax.random.key(seed), 5)
    return {
        "fields": gaussian(keys[0], (V, NS, G), 1.0, 6.0, ((0, 4), (2, 32))),
        "eigenfunctions": gaussian(keys[1], (V, M, G), G ** -0.5, 0.015625, ((0, 4), (2, 32))),
        "start": gaussian(keys[2], (JD, K), 1.0, 6.0, (), jnp.float32),
        "grid_count": with_ends(jax.random.randint(keys[3], (V,), G // 2, G + 1), jax.random.fold_in(keys[3], 1), G // 2, G).astype(jnp.int32),
    }


def orthogonalize(image):
    gram = jnp.dot(image.T.astype(jnp.float32), image.astype(jnp.float32), precision=lax.Precision.HIGHEST, preferred_element_type=jnp.float32)
    lower = jnp.linalg.cholesky(gram)
    return jax.scipy.linalg.solve_triangular(lower, image.T, lower=True).T

def reference(fields, eigenfunctions, start, grid_count):
    points = jnp.arange(G, dtype=jnp.int32)
    valid = points[None, :] < grid_count[:, None]
    masked = jnp.where(valid[:, None, :], eigenfunctions, jnp.zeros((), eigenfunctions.dtype))

    def project(pair):
        return jnp.dot(pair[0].astype(jnp.float32), pair[1].T.astype(jnp.float32), preferred_element_type=jnp.float32)
    scores = lax.map(project, (fields, masked))
    joint = jnp.transpose(scores, (1, 0, 2)).reshape(NS, V * M)
    centred = joint - jnp.mean(joint, axis=0, keepdims=True)
    cov = jnp.dot(centred.T.astype(jnp.float32), centred.astype(jnp.float32), precision=lax.Precision.HIGHEST, preferred_element_type=jnp.float32) / (NS - 1)
    basis = start
    for sweep in range(SWEEPS):
        image = jnp.dot(cov.astype(jnp.float32), basis.astype(jnp.float32), precision=lax.Precision.HIGHEST, preferred_element_type=jnp.float32)
        basis = orthogonalize(image)
    component_scores = jnp.dot(centred.astype(jnp.float32), basis.astype(jnp.float32), precision=lax.Precision.HIGHEST, preferred_element_type=jnp.float32)
    basis_low = basis.astype(jnp.bfloat16).reshape(V, M, K)
    scores_low = component_scores.astype(jnp.bfloat16)

    def rebuild(trio):
        values, funcs, coeffs = trio
        loading = jnp.dot(coeffs.T.astype(jnp.float32), funcs.astype(jnp.float32), preferred_element_type=jnp.float32).astype(jnp.bfloat16)
        rebuilt = jnp.dot(scores_low.astype(jnp.float32), loading.astype(jnp.float32), preferred_element_type=jnp.float32)
        wide = values.astype(jnp.float32)
        deviation = wide - jnp.mean(wide, axis=0, keepdims=True)
        gain = jnp.sum(2.0 * deviation * rebuilt - rebuilt * rebuilt, axis=1) / M
        return (loading, gain)
    loadings, explained = lax.map(rebuild, (fields, masked, basis_low))
    return (loadings, component_scores, explained)
```

```python
import jax
import jax.numpy as jnp
from jax import lax
from jax.experimental import pallas as pl
from jax.experimental.pallas import tpu as pltpu
from jax.sharding import Mesh, PartitionSpec as P

M = 64
K = 128
SWEEPS = 2
HIGHEST = lax.Precision.HIGHEST
F32 = jnp.float32
BF16 = jnp.bfloat16
STEP = 512


def dot(left, right, lc, rc, precision=None):
    return lax.dot_general(
        left, right, (((lc,), (rc,)), ((), ())), precision=precision, preferred_element_type=F32
    )


def masked_part(e, first, count):
    columns = first + lax.broadcasted_iota(jnp.int32, e.shape, 1)
    return jnp.where(columns < count, e.astype(F32), 0.0).astype(BF16)


def local_counts(count_ref, points):
    var = lax.axis_index("zh") * lax.axis_size("core") + lax.axis_index("core")
    first = lax.axis_index("space") * points
    return count_ref[2 * var] - first, count_ref[2 * var + 1] - first


def project_kernel(points, peers, count_ref, f_ref, e_ref, out_ref, acc_ref):
    step = pl.program_id(0)
    count0, count1 = local_counts(count_ref, points)
    samples = f_ref.shape[1]
    width = f_ref.shape[2]
    e0 = masked_part(e_ref[0], step * width, count0)
    e1 = masked_part(e_ref[1], step * width, count1)
    none = jnp.zeros_like(e0)
    right0 = jnp.concatenate([e0, none], axis=0)
    right1 = jnp.concatenate([none, e1], axis=0)

    @pl.when(step == 0)
    def _():
        acc_ref[...] = jnp.zeros_like(acc_ref)

    acc_ref[:samples] += dot(f_ref[0], right0, 1, 1) + dot(f_ref[1], right1, 1, 1)
    acc_ref[samples:] += dot(e0, right0, 1, 1) + dot(e1, right1, 1, 1)

    @pl.when(step == pl.num_programs(0) - 1)
    def _():
        own, extra = samples // peers, M // peers
        size = own + extra
        for peer in range(peers):
            out_ref[peer * size : peer * size + own] = acc_ref[peer * own : (peer + 1) * own]
            out_ref[peer * size + own : (peer + 1) * size] = acc_ref[
                samples + peer * extra : samples + (peer + 1) * extra
            ]


def project(fields, eigenfunctions, grid_count, peers):
    _, samples, points = fields.shape
    rows = samples + M
    return pl.pallas_call(
        lambda *refs: project_kernel(points, peers, *refs),
        name="project",
        out_shape=jax.ShapeDtypeStruct((rows, 2 * M), F32),
        grid_spec=pltpu.PrefetchScalarGridSpec(
            num_scalar_prefetch=1,
            grid=(points // STEP,),
            in_specs=[
                pl.BlockSpec((2, samples, STEP), lambda i, c: (0, 0, i)),
                pl.BlockSpec((2, M, STEP), lambda i, c: (0, 0, i)),
            ],
            out_specs=pl.BlockSpec((rows, 2 * M), lambda i, c: (0, 0)),
            scratch_shapes=[pltpu.VMEM((rows, 2 * M), F32)],
        ),
        compiler_params=pltpu.CompilerParams(
            dimension_semantics=("arbitrary",), vmem_limit_bytes=32 << 20
        ),
    )(grid_count, fields, eigenfunctions)


def inverse_factor(gram):
    size = gram.shape[0]
    tiles = size // 8
    row = lax.broadcasted_iota(jnp.int32, (8, size), 0)
    column = lax.broadcasted_iota(jnp.int32, (8, size), 1)
    left = [gram[8 * i : 8 * i + 8] for i in range(tiles)]
    made = [jnp.where(row + 8 * i == column, 1.0, 0.0).astype(F32) for i in range(tiles)]
    for j in range(size):
        k, s = divmod(j, 8)
        pivot = left[k][s : s + 1, j : j + 1]
        inverse = 1.0 / pivot
        own = made[k][s : s + 1]
        scaled = left[k][s : s + 1] * inverse
        scaled_own = own * inverse
        for i in range(k, tiles):
            factor = left[i][:, j : j + 1]
            if i == k:
                if s == 7:
                    continue
                factor = jnp.where(row[:, :1] > s, factor, 0.0)
            left[i] = left[i] - factor * scaled
            made[i] = made[i] - factor * scaled_own
        made[k] = jnp.where(row == s, own * lax.rsqrt(pivot), made[k])
    return jnp.concatenate(made, axis=0)


def solve_kernel(
    points, peers, count_ref, mine_ref, other_ref, start_ref, e_ref,
    load_ref, score_ref, gain_ref, c_ref, cov_ref, held_ref, sem,
):
    samples = score_ref.shape[0]
    own, extra = samples // peers, M // peers
    size = own + extra
    core, zh = lax.axis_index("core"), lax.axis_index("zh")
    for source, ref in ((core, mine_ref), (1 - core, other_ref)):
        for half in range(2):
            base = half * peers * size
            block = jnp.concatenate(
                [ref[base + p * size : base + p * size + own] for p in range(peers)], axis=0
            )
            mean = jnp.sum(block, axis=0, keepdims=True) / samples
            place = pl.multiple_of((half * 2 + source) * 2 * M, 2 * M)
            c_ref[:, pl.ds(place, 2 * M)] = block - mean
    centred = c_ref[...]
    cov = dot(centred, centred, 0, 0, HIGHEST) / (samples - 1)
    cov_ref[...] = cov
    basis = start_ref[...]
    for _ in range(SWEEPS):
        image = dot(cov_ref[...], basis, 1, 0, HIGHEST)
        gram = dot(image, image, 0, 0, HIGHEST)
        basis = dot(image, inverse_factor(gram), 1, 1, HIGHEST)
    held_ref[...] = basis
    var = zh * 2 + core
    first = pl.multiple_of(var * 2 * M, 2 * M)
    low = held_ref[pl.ds(first, 2 * M)].astype(BF16)
    counts = local_counts(count_ref, points)
    width = STEP
    copies = []
    for v in range(2):
        for at in range(0, points, width):
            e = masked_part(e_ref[v, :, at : at + width], at, counts[v])
            load_ref_v = dot(low[v * M : (v + 1) * M], e, 0, 0).astype(BF16)
            load_ref[v, :, at : at + width] = load_ref_v
    scores = dot(c_ref[...], held_ref[...], 1, 0, HIGHEST)
    score_ref[...] = scores
    scores_low = scores.astype(BF16).astype(F32)
    base = zh * peers * size
    for v in range(2):
        outer = jnp.concatenate(
            [
                mine_ref[pl.ds(base + p * size + own, extra), v * M : (v + 1) * M]
                for p in range(peers)
            ],
            axis=0,
        )
        part = low[v * M : (v + 1) * M].astype(F32)
        square = dot(part, dot(outer, part, 1, 0, HIGHEST), 0, 0, HIGHEST)
        along = dot(c_ref[:, pl.ds(first, 2 * M)][:, v * M : (v + 1) * M], part, 1, 0, HIGHEST)
        both = scores_low * (2.0 * along - dot(scores_low, square, 1, 0, HIGHEST))
        ones = jnp.ones((8, K), F32)
        gain_ref[v : v + 1] = dot(ones, both, 1, 1, HIGHEST)[:1] / M


def solve(grid_count, mine, other, start, eigenfunctions, samples, peers):
    points = eigenfunctions.shape[2]
    joint = start.shape[0]
    vmem = pl.BlockSpec(memory_space=pltpu.VMEM)
    return pl.pallas_call(
        lambda *refs: solve_kernel(points, peers, *refs),
        name="solve",
        out_shape=(
            jax.ShapeDtypeStruct((2, K, points), BF16),
            jax.ShapeDtypeStruct((samples, K), F32),
            jax.ShapeDtypeStruct((2, samples), F32),
        ),
        in_specs=[pl.BlockSpec(memory_space=pltpu.SMEM), vmem, vmem, vmem, vmem],
        out_specs=(vmem, vmem, vmem),
        scratch_shapes=[
            pltpu.VMEM((samples, joint), F32),
            pltpu.VMEM((joint, joint), F32),
            pltpu.VMEM((joint, K), F32),
            pltpu.SemaphoreType.DMA,
        ],
        compiler_params=pltpu.CompilerParams(vmem_limit_bytes=48 << 20),
    )(grid_count, mine, other, start, eigenfunctions)


def shards(fields, eigenfunctions, start, grid_count):
    samples = fields.shape[1]
    peers = lax.axis_size("space")
    part = project(fields, eigenfunctions, grid_count, peers)
    length = part.size // peers
    tiles = lax.all_to_all(part.reshape(peers, 1, length), "space", 0, 0, tiled=True)
    tile = jnp.sum(tiles, axis=0)
    group = ("zh", "space")
    copies = jnp.broadcast_to(tile, (2 * peers, 1, length))
    mine = lax.all_to_all(copies, group, 0, 0, tiled=True).reshape(-1, 2 * M)
    other = lax.ppermute(mine, "core", ((0, 1), (1, 0)))
    return solve(grid_count, mine, other, start, eigenfunctions, samples, peers)


def solution(mesh):
    var, space = mesh.devices.shape
    finer = Mesh(mesh.devices.reshape(var // 2, 2, space), ("zh", "core", "space"))
    split = P(("zh", "core"), None, "space")
    return jax.shard_map(
        shards,
        mesh=finer,
        in_specs=(split, split, P(), P()),
        out_specs=(split, P(), P(("zh", "core"), None)),
        check_vma=False,
    )
```

```python
import jax
import jax.numpy as jnp
from jax import lax
from jax.experimental import pallas as pl
from jax.experimental.pallas import tpu as pltpu
from jax.sharding import Mesh, PartitionSpec as P

M = 64
K = 128
SWEEPS = 2
HIGHEST = lax.Precision.HIGHEST
F32 = jnp.float32
BF16 = jnp.bfloat16
STEP = 1024


def dot(left, right, lc, rc, precision=None):
    return lax.dot_general(
        left, right, (((lc,), (rc,)), ((), ())), precision=precision, preferred_element_type=F32
    )


def masked_part(e, first, count):
    columns = first + lax.broadcasted_iota(jnp.int32, e.shape, 1)
    return jnp.where(columns < count, e.astype(F32), 0.0).astype(BF16)


def local_counts(count_ref, points):
    var = lax.axis_index("zh") * lax.axis_size("core") + lax.axis_index("core")
    first = lax.axis_index("space") * points
    return count_ref[2 * var] - first, count_ref[2 * var + 1] - first


def project_kernel(points, peers, count_ref, f_ref, e_ref, out_ref, acc_ref):
    step = pl.program_id(0)
    count0, count1 = local_counts(count_ref, points)
    samples = f_ref.shape[1]
    width = f_ref.shape[2]
    e0 = masked_part(e_ref[0], step * width, count0)
    e1 = masked_part(e_ref[1], step * width, count1)
    none = jnp.zeros_like(e0)
    right0 = jnp.concatenate([e0, none], axis=0)
    right1 = jnp.concatenate([none, e1], axis=0)

    @pl.when(step == 0)
    def _():
        acc_ref[...] = jnp.zeros_like(acc_ref)

    acc_ref[:samples] += dot(f_ref[0], right0, 1, 1) + dot(f_ref[1], right1, 1, 1)
    acc_ref[samples:] += dot(e0, right0, 1, 1) + dot(e1, right1, 1, 1)

    @pl.when(step == pl.num_programs(0) - 1)
    def _():
        own, extra = samples // peers, M // peers
        size = own + extra
        for peer in range(peers):
            out_ref[peer * size : peer * size + own] = acc_ref[peer * own : (peer + 1) * own]
            out_ref[peer * size + own : (peer + 1) * size] = acc_ref[
                samples + peer * extra : samples + (peer + 1) * extra
            ]


def project(fields, eigenfunctions, grid_count, peers):
    _, samples, points = fields.shape
    rows = samples + M
    return pl.pallas_call(
        lambda *refs: project_kernel(points, peers, *refs),
        name="project",
        out_shape=jax.ShapeDtypeStruct((rows, 2 * M), F32),
        grid_spec=pltpu.PrefetchScalarGridSpec(
            num_scalar_prefetch=1,
            grid=(points // STEP,),
            in_specs=[
                pl.BlockSpec((2, samples, STEP), lambda i, c: (0, 0, i)),
                pl.BlockSpec((2, M, STEP), lambda i, c: (0, 0, i)),
            ],
            out_specs=pl.BlockSpec((rows, 2 * M), lambda i, c: (0, 0)),
            scratch_shapes=[pltpu.VMEM((rows, 2 * M), F32)],
        ),
        compiler_params=pltpu.CompilerParams(
            dimension_semantics=("arbitrary",), vmem_limit_bytes=60 << 20
        ),
    )(grid_count, fields, eigenfunctions)


def halves(x):
    high = x.astype(BF16)
    return high, (x - high.astype(F32)).astype(BF16)


def thirds(x):
    high, rest = x.astype(BF16), x
    rest = rest - high.astype(F32)
    middle = rest.astype(BF16)
    return high, middle, (rest - middle.astype(F32)).astype(BF16)


def folded(x):
    half = x.shape[1] // 2
    return x[:, :half] + x[:, half:]


def product(left, x):
    pair = jnp.concatenate(halves(x), axis=1)
    return folded(dot(left, jnp.concatenate([pair, pair], axis=0), 1, 0))


def gram_of(image):
    high, middle, low = thirds(image)
    pair = jnp.concatenate([high, middle], axis=1)
    main = folded(
        dot(jnp.concatenate([high, middle], axis=0), jnp.concatenate([pair, pair], axis=0), 0, 0)
    )
    last = dot(high, low, 0, 0)
    return main + (last + last.T)


def times_transposed(image, factor):
    high, middle, low = thirds(image)
    f_high, f_middle, f_low = thirds(factor)
    right = jnp.concatenate(
        [jnp.concatenate([f_high] * 2, axis=1), jnp.concatenate([f_middle] * 2, axis=1)], axis=0
    )
    main = folded(dot(jnp.concatenate([high, middle], axis=1), right, 1, 1))
    return main + dot(
        jnp.concatenate([high, low], axis=1), jnp.concatenate([f_low, f_high], axis=1), 1, 1
    )


def inverse_factor(gram, left_ref, made_ref, out_ref):
    size = gram.shape[0]
    wide = (8, size)
    row = lax.broadcasted_iota(jnp.int32, wide, 0)
    left_ref[...] = gram
    made_ref[...] = jnp.where(
        lax.broadcasted_iota(jnp.int32, (size, size), 0)
        == lax.broadcasted_iota(jnp.int32, (size, size), 1),
        1.0,
        0.0,
    ).astype(F32)
    for first in range(0, size, 16):
        tiles = (first, first + 8)
        left = [left_ref[t : t + 8] for t in tiles]
        made = [made_ref[t : t + 8] for t in tiles]
        spread = [
            [jnp.broadcast_to(x[:, first + j : first + j + 1], wide) for j in range(16)]
            for x in left
        ]
        scale = [jnp.ones(wide, F32)] * 2
        for j in range(16):
            tile, s = divmod(j, 8)
            root = lax.rsqrt(jnp.broadcast_to(spread[tile][j][s : s + 1], wide))
            scale[tile] = jnp.where(row == s, root, scale[tile])
            inverse = root * root
            factor = {}
            for t in range(tile, 2):
                factor[t] = spread[t][j] * inverse
            factor[tile] = jnp.where(row > s, factor[tile], 0.0)
            for other in range(j + 1, 16):
                pivot_row = jnp.broadcast_to(spread[tile][other][s : s + 1], wide)
                for t in factor:
                    spread[t][other] = spread[t][other] - factor[t] * pivot_row
            left_row = jnp.broadcast_to(left[tile][s : s + 1], wide)
            made_row = jnp.broadcast_to(made[tile][s : s + 1], wide)
            for t in factor:
                left[t] = left[t] - factor[t] * left_row
                made[t] = made[t] - factor[t] * made_row
        upper = jnp.concatenate([left[t] * scale[t] for t in range(2)], axis=0)
        done = jnp.concatenate([made[t] * scale[t] for t in range(2)], axis=0)
        out_ref[first : first + 16] = done
        rest = first + 16
        if rest < size:
            a, b, c = thirds(upper)
            d, e, f = thirds(jnp.concatenate([upper, done], axis=1))
            update = dot(
                jnp.concatenate([a, a, b, b, a, c], axis=0),
                jnp.concatenate([d, e, d, e, f, d], axis=0),
                0,
                0,
            )
            left_ref[rest:] = left_ref[rest:] - update[rest:, :size]
            made_ref[rest:] = made_ref[rest:] - update[rest:, size:]
    return out_ref[...]


def solve_kernel(
    points, peers, count_ref, mine_ref, other_ref, start_ref, e_ref,
    load_ref, score_ref, gain_ref,
    high_ref, middle_ref, cov_ref, held_ref, left_ref, made_ref, factor_ref, out_ref, sem,
):
    samples = score_ref.shape[0]
    joint = start_ref.shape[0]
    own, extra = samples // peers, M // peers
    size = own + extra
    pair = 2 * M
    core, zh = lax.axis_index("core"), lax.axis_index("zh")
    for source, ref in ((core, mine_ref), (1 - core, other_ref)):
        for half in range(2):
            base = half * peers * size
            block = jnp.concatenate(
                [ref[base + p * size : base + p * size + own] for p in range(peers)], axis=0
            )
            mean = jnp.sum(block, axis=0, keepdims=True) / samples
            place = pl.ds(pl.multiple_of((half * 2 + source) * pair, pair), pair)
            high_ref[:, place], middle_ref[:, place] = halves(block - mean)
    high, middle = high_ref[...], middle_ref[...]
    main = dot(high, high, 0, 0)
    cross = dot(high, middle, 0, 0)
    cov = (main + (cross + cross.T)) * (1.0 / (samples - 1))
    cov_ref[:, :joint], cov_ref[:, joint:] = halves(cov)
    basis = start_ref[...]
    for _ in range(SWEEPS):
        image = product(cov_ref[...], basis)
        factor = inverse_factor(gram_of(image), left_ref, made_ref, factor_ref)
        basis = times_transposed(image, factor)
    held_ref[...] = basis
    first = pl.multiple_of((zh * 2 + core) * pair, pair)
    low = held_ref[pl.ds(first, pair)].astype(BF16)
    counts = local_counts(count_ref, points)
    copies = []
    for at in range(0, points, STEP):
        for v in range(2):
            e = masked_part(e_ref[v, :, at : at + STEP], at, counts[v])
            out_ref[v, :, at : at + STEP] = dot(low[v * M : (v + 1) * M], e, 0, 0).astype(BF16)
        part = (slice(None), slice(None), slice(at, at + STEP))
        copy = pltpu.make_async_copy(out_ref.at[part], load_ref.at[part], sem.at[at // STEP])
        copy.start()
        copies.append(copy)
    scores = product(jnp.concatenate([high_ref[...], middle_ref[...]], axis=1), basis)
    score_ref[...] = scores
    scores_low = scores.astype(BF16)
    base = zh * peers * size
    outer = jnp.concatenate(
        [mine_ref[pl.ds(base + p * size + own, extra)] for p in range(peers)], axis=0
    )
    row = lax.broadcasted_iota(jnp.int32, (pair, pair), 0) // M
    column = lax.broadcasted_iota(jnp.int32, (pair, pair), 1) // M
    outer = jnp.where(row == column, jnp.concatenate([outer, outer], axis=0), 0.0)
    row = lax.broadcasted_iota(jnp.int32, (pair, 2 * K), 0) // M
    column = lax.broadcasted_iota(jnp.int32, (pair, 2 * K), 1) // K
    wide = low.astype(F32)
    blocks = jnp.where(row == column, jnp.concatenate([wide, wide], axis=1), 0.0)
    square = dot(wide, dot(outer, blocks, 1, 0, HIGHEST), 0, 0, HIGHEST)
    square_high, square_middle = halves(-square)
    twice = (2.0 * blocks).astype(BF16)
    place = pl.ds(first, pair)
    along = dot(
        jnp.concatenate(
            [high_ref[:, place], middle_ref[:, place], scores_low, scores_low], axis=1
        ),
        jnp.concatenate([twice, twice, square_high, square_middle], axis=0),
        1,
        0,
    )
    wide_scores = scores_low.astype(F32)
    both_high, both_middle = halves(along * jnp.concatenate([wide_scores, wide_scores], axis=1))
    chosen = lax.broadcasted_iota(jnp.int32, (8, 2 * K), 0)
    chosen = chosen == lax.broadcasted_iota(jnp.int32, (8, 2 * K), 1) // K
    chosen = jnp.where(chosen, 1.0, 0.0).astype(BF16)
    gain = dot(chosen, both_high, 1, 1) + dot(chosen, both_middle, 1, 1)
    gain_ref[...] = gain[:2] / M
    for copy in copies:
        copy.wait()


def solve(grid_count, mine, other, start, eigenfunctions, samples, peers):
    points = eigenfunctions.shape[2]
    joint = start.shape[0]
    vmem = pl.BlockSpec(memory_space=pltpu.VMEM)
    return pl.pallas_call(
        lambda *refs: solve_kernel(points, peers, *refs),
        name="solve",
        out_shape=(
            jax.ShapeDtypeStruct((2, K, points), BF16),
            jax.ShapeDtypeStruct((samples, K), F32),
            jax.ShapeDtypeStruct((2, samples), F32),
        ),
        in_specs=[pl.BlockSpec(memory_space=pltpu.SMEM), vmem, vmem, vmem, vmem],
        out_specs=(pl.BlockSpec(memory_space=pl.ANY), vmem, vmem),
        scratch_shapes=[
            pltpu.VMEM((samples, joint), BF16),
            pltpu.VMEM((samples, joint), BF16),
            pltpu.VMEM((joint, 2 * joint), BF16),
            pltpu.VMEM((joint, K), F32),
            pltpu.VMEM((K, K), F32),
            pltpu.VMEM((K, K), F32),
            pltpu.VMEM((K, K), F32),
            pltpu.VMEM((2, K, points), BF16),
            pltpu.SemaphoreType.DMA((points // STEP,)),
        ],
        compiler_params=pltpu.CompilerParams(vmem_limit_bytes=40 << 20),
    )(grid_count, mine, other, start, eigenfunctions)


def shards(fields, eigenfunctions, start, grid_count):
    samples = fields.shape[1]
    peers = lax.axis_size("space")
    part = project(fields, eigenfunctions, grid_count, peers)
    length = part.size // peers
    tiles = lax.all_to_all(part.reshape(peers, 1, length), "space", 0, 0, tiled=True)
    tile = jnp.sum(tiles, axis=0)
    group = ("zh", "space")
    copies = jnp.broadcast_to(tile, (2 * peers, 1, length))
    mine = lax.all_to_all(copies, group, 0, 0, tiled=True).reshape(-1, 2 * M)
    other = lax.ppermute(mine, "core", ((0, 1), (1, 0)))
    return solve(grid_count, mine, other, start, eigenfunctions, samples, peers)


def solution(mesh):
    var, space = mesh.devices.shape
    finer = Mesh(mesh.devices.reshape(var // 2, 2, space), ("zh", "core", "space"))
    split = P(("zh", "core"), None, "space")
    return jax.shard_map(
        shards,
        mesh=finer,
        in_specs=(split, split, P(), P()),
        out_specs=(split, P(), P(("zh", "core"), None)),
        check_vma=False,
    )
```

```python
import jax
import jax.numpy as jnp
from jax import lax
from jax.experimental import pallas as pl
from jax.experimental.pallas import tpu as pltpu
from jax.sharding import Mesh, PartitionSpec as P

M = 64
K = 128
SWEEPS = 2
HIGHEST = lax.Precision.HIGHEST
F32 = jnp.float32
BF16 = jnp.bfloat16
STEP = 1024


def dot(left, right, lc, rc, precision=None):
    return lax.dot_general(
        left, right, (((lc,), (rc,)), ((), ())), precision=precision, preferred_element_type=F32
    )


def masked_part(e, first, count):
    columns = first + lax.broadcasted_iota(jnp.int32, e.shape, 1)
    return jnp.where(columns < count, e.astype(F32), 0.0).astype(BF16)


def local_counts(count_ref, points):
    var = lax.axis_index("zh") * lax.axis_size("core") + lax.axis_index("core")
    first = lax.axis_index("space") * points
    return count_ref[2 * var] - first, count_ref[2 * var + 1] - first


def project_kernel(points, peers, count_ref, f_ref, e_ref, out_ref, acc_ref):
    step = pl.program_id(0)
    count0, count1 = local_counts(count_ref, points)
    samples = f_ref.shape[1]
    width = f_ref.shape[2]
    e0 = masked_part(e_ref[0], step * width, count0)
    e1 = masked_part(e_ref[1], step * width, count1)
    none = jnp.zeros_like(e0)
    right0 = jnp.concatenate([e0, none], axis=0)
    right1 = jnp.concatenate([none, e1], axis=0)

    @pl.when(step == 0)
    def _():
        acc_ref[...] = jnp.zeros_like(acc_ref)

    acc_ref[:samples] += dot(f_ref[0], right0, 1, 1) + dot(f_ref[1], right1, 1, 1)
    acc_ref[samples:] += dot(e0, right0, 1, 1) + dot(e1, right1, 1, 1)

    @pl.when(step == pl.num_programs(0) - 1)
    def _():
        own, extra = samples // peers, M // peers
        size = own + extra
        for peer in range(peers):
            out_ref[peer * size : peer * size + own] = acc_ref[peer * own : (peer + 1) * own]
            out_ref[peer * size + own : (peer + 1) * size] = acc_ref[
                samples + peer * extra : samples + (peer + 1) * extra
            ]


def project(fields, eigenfunctions, grid_count, peers):
    _, samples, points = fields.shape
    rows = samples + M
    return pl.pallas_call(
        lambda *refs: project_kernel(points, peers, *refs),
        name="project",
        out_shape=jax.ShapeDtypeStruct((rows, 2 * M), F32),
        grid_spec=pltpu.PrefetchScalarGridSpec(
            num_scalar_prefetch=1,
            grid=(points // STEP,),
            in_specs=[
                pl.BlockSpec((2, samples, STEP), lambda i, c: (0, 0, i)),
                pl.BlockSpec((2, M, STEP), lambda i, c: (0, 0, i)),
            ],
            out_specs=pl.BlockSpec((rows, 2 * M), lambda i, c: (0, 0)),
            scratch_shapes=[pltpu.VMEM((rows, 2 * M), F32)],
        ),
        compiler_params=pltpu.CompilerParams(
            dimension_semantics=("arbitrary",), vmem_limit_bytes=60 << 20
        ),
    )(grid_count, fields, eigenfunctions)


def halves(x):
    high = x.astype(BF16)
    return high, (x - high.astype(F32)).astype(BF16)


def thirds(x):
    high, rest = x.astype(BF16), x
    rest = rest - high.astype(F32)
    middle = rest.astype(BF16)
    return high, middle, (rest - middle.astype(F32)).astype(BF16)


def folded(x):
    half = x.shape[1] // 2
    return x[:, :half] + x[:, half:]


def pair_up(x):
    return jnp.concatenate(halves(x), axis=1)


def product(left, pair):
    return folded(dot(left, jnp.concatenate([pair, pair], axis=0), 1, 0))


def gram_of(image):
    high, middle, low = thirds(image)
    pair = jnp.concatenate([high, middle], axis=1)
    main = folded(
        dot(jnp.concatenate([high, middle], axis=0), jnp.concatenate([pair, pair], axis=0), 0, 0)
    )
    last = dot(high, low, 0, 0)
    return main + (last + last.T)


def times_transposed(image, factor):
    high, middle, low = thirds(image)
    f_high, f_middle, f_low = thirds(factor)
    right = jnp.concatenate(
        [jnp.concatenate([f_high] * 2, axis=1), jnp.concatenate([f_middle] * 2, axis=1)], axis=0
    )
    main = folded(dot(jnp.concatenate([high, middle], axis=1), right, 1, 1))
    return main + dot(
        jnp.concatenate([high, low], axis=1), jnp.concatenate([f_low, f_high], axis=1), 1, 1
    )


def inverse_factor(gram, left_ref, made_ref, out_ref):
    size = gram.shape[0]
    wide = (8, size)
    row = lax.broadcasted_iota(jnp.int32, wide, 0)
    left_ref[...] = gram
    made_ref[...] = jnp.where(
        lax.broadcasted_iota(jnp.int32, (size, size), 0)
        == lax.broadcasted_iota(jnp.int32, (size, size), 1),
        1.0,
        0.0,
    ).astype(F32)
    for first in range(0, size, 16):
        tiles = (first, first + 8)
        left = [left_ref[t : t + 8] for t in tiles]
        made = [made_ref[t : t + 8] for t in tiles]
        spread = [
            [jnp.broadcast_to(x[:, first + j : first + j + 1], wide) for j in range(16)]
            for x in left
        ]
        scale = [jnp.ones(wide, F32)] * 2
        for j in range(16):
            tile, s = divmod(j, 8)
            root = lax.rsqrt(jnp.broadcast_to(spread[tile][j][s : s + 1], wide))
            scale[tile] = jnp.where(row == s, root, scale[tile])
            inverse = root * root
            factor = {}
            for t in range(tile, 2):
                factor[t] = spread[t][j] * inverse
            factor[tile] = jnp.where(row > s, factor[tile], 0.0)
            for other in range(j + 1, 16):
                pivot_row = jnp.broadcast_to(spread[tile][other][s : s + 1], wide)
                for t in factor:
                    spread[t][other] = spread[t][other] - factor[t] * pivot_row
            left_row = jnp.broadcast_to(left[tile][s : s + 1], wide)
            made_row = jnp.broadcast_to(made[tile][s : s + 1], wide)
            for t in factor:
                left[t] = left[t] - factor[t] * left_row
                made[t] = made[t] - factor[t] * made_row
        upper = jnp.concatenate([left[t] * scale[t] for t in range(2)], axis=0)
        done = jnp.concatenate([made[t] * scale[t] for t in range(2)], axis=0)
        out_ref[first : first + 16] = done
        rest = first + 16
        if rest < size:
            a, b, c = thirds(upper)
            d, e, f = thirds(jnp.concatenate([upper, done], axis=1))
            update = dot(
                jnp.concatenate([a, a, b, b, a, c], axis=0),
                jnp.concatenate([d, e, d, e, f, d], axis=0),
                0,
                0,
            )
            left_ref[rest:] = left_ref[rest:] - update[rest:, :size]
            made_ref[rest:] = made_ref[rest:] - update[rest:, size:]
    return out_ref[...]


def solve_kernel(
    points, peers, mine_ref, other_ref, start_ref, e_ref,
    load_ref, score_ref, gain_ref,
    high_ref, middle_ref, cov_ref, held_ref, left_ref, made_ref, factor_ref, out_ref, sem,
):
    samples = score_ref.shape[0]
    joint = start_ref.shape[0]
    own, extra = samples // peers, M // peers
    size = own + extra
    pair = 2 * M
    core, zh = lax.axis_index("core"), lax.axis_index("zh")
    for source, ref in ((core, mine_ref), (1 - core, other_ref)):
        for half in range(2):
            base = half * peers * size
            block = jnp.concatenate(
                [ref[base + p * size : base + p * size + own] for p in range(peers)], axis=0
            )
            mean = jnp.sum(block, axis=0, keepdims=True) / samples
            place = pl.ds(pl.multiple_of((half * 2 + source) * pair, pair), pair)
            high_ref[:, place], middle_ref[:, place] = halves(block - mean)
    high, middle = high_ref[...], middle_ref[...]
    main = dot(high, high, 0, 0)
    cross = dot(high, middle, 0, 0)
    cov = (main + (cross + cross.T)) * (1.0 / (samples - 1))
    cov_ref[:, :joint], cov_ref[:, joint:] = halves(cov)
    basis_pair = start_ref[...]
    for _ in range(SWEEPS):
        image = product(cov_ref[...], basis_pair)
        factor = inverse_factor(gram_of(image), left_ref, made_ref, factor_ref)
        basis = times_transposed(image, factor)
        basis_pair = pair_up(basis)
    held_ref[...] = basis
    first = pl.multiple_of((zh * 2 + core) * pair, pair)
    low = held_ref[pl.ds(first, pair)].astype(BF16)
    copies = []
    for at in range(0, points, STEP):
        for v in range(2):
            e = e_ref[v, :, at : at + STEP]
            out_ref[v, :, at : at + STEP] = dot(low[v * M : (v + 1) * M], e, 0, 0).astype(BF16)
        part = (slice(None), slice(None), slice(at, at + STEP))
        copy = pltpu.make_async_copy(out_ref.at[part], load_ref.at[part], sem.at[at // STEP])
        copy.start()
        copies.append(copy)
    scores = product(jnp.concatenate([high_ref[...], middle_ref[...]], axis=1), basis_pair)
    score_ref[...] = scores
    scores_low = scores.astype(BF16)
    base = zh * peers * size
    outer = jnp.concatenate(
        [mine_ref[pl.ds(base + p * size + own, extra)] for p in range(peers)], axis=0
    )
    row = lax.broadcasted_iota(jnp.int32, (pair, pair), 0) // M
    column = lax.broadcasted_iota(jnp.int32, (pair, pair), 1) // M
    outer = jnp.where(row == column, jnp.concatenate([outer, outer], axis=0), 0.0)
    row = lax.broadcasted_iota(jnp.int32, (pair, 2 * K), 0) // M
    column = lax.broadcasted_iota(jnp.int32, (pair, 2 * K), 1) // K
    wide = low.astype(F32)
    blocks = jnp.where(row == column, jnp.concatenate([wide, wide], axis=1), 0.0)
    square = dot(wide, dot(outer, blocks, 1, 0, HIGHEST), 0, 0, HIGHEST)
    square_high, square_middle = halves(-square)
    twice = (2.0 * blocks).astype(BF16)
    place = pl.ds(first, pair)
    along = dot(
        jnp.concatenate(
            [high_ref[:, place], middle_ref[:, place], scores_low, scores_low], axis=1
        ),
        jnp.concatenate([twice, twice, square_high, square_middle], axis=0),
        1,
        0,
    )
    wide_scores = scores_low.astype(F32)
    both_high, both_middle = halves(along * jnp.concatenate([wide_scores, wide_scores], axis=1))
    chosen = lax.broadcasted_iota(jnp.int32, (8, 2 * K), 0)
    chosen = chosen == lax.broadcasted_iota(jnp.int32, (8, 2 * K), 1) // K
    chosen = jnp.where(chosen, 1.0, 0.0).astype(BF16)
    gain = dot(chosen, both_high, 1, 1) + dot(chosen, both_middle, 1, 1)
    gain_ref[...] = gain[:2] / M
    for copy in copies:
        copy.wait()


def solve(mine, other, start, masked, samples, peers):
    points = masked.shape[2]
    joint = start.shape[0]
    vmem = pl.BlockSpec(memory_space=pltpu.VMEM)
    return pl.pallas_call(
        lambda *refs: solve_kernel(points, peers, *refs),
        name="solve",
        out_shape=(
            jax.ShapeDtypeStruct((2, K, points), BF16),
            jax.ShapeDtypeStruct((samples, K), F32),
            jax.ShapeDtypeStruct((2, samples), F32),
        ),
        in_specs=[vmem] * 4,
        out_specs=(pl.BlockSpec(memory_space=pl.ANY), vmem, vmem),
        scratch_shapes=[
            pltpu.VMEM((samples, joint), BF16),
            pltpu.VMEM((samples, joint), BF16),
            pltpu.VMEM((joint, 2 * joint), BF16),
            pltpu.VMEM((joint, K), F32),
            pltpu.VMEM((K, K), F32),
            pltpu.VMEM((K, K), F32),
            pltpu.VMEM((K, K), F32),
            pltpu.VMEM((2, K, points), BF16),
            pltpu.SemaphoreType.DMA((points // STEP,)),
        ],
        compiler_params=pltpu.CompilerParams(vmem_limit_bytes=40 << 20),
    )(mine, other, start, masked)


def mask_kernel(points, count_ref, e_ref, after_ref, out_ref):
    counts = local_counts(count_ref, points)
    for v in range(2):
        out_ref[v] = masked_part(e_ref[v], 0, counts[v])


def mask(grid_count, eigenfunctions, after):
    vmem = pl.BlockSpec(memory_space=pltpu.VMEM)
    points = eigenfunctions.shape[2]
    return pl.pallas_call(
        lambda *refs: mask_kernel(points, *refs),
        name="mask",
        out_shape=jax.ShapeDtypeStruct(eigenfunctions.shape, BF16),
        in_specs=[pl.BlockSpec(memory_space=pltpu.SMEM), vmem, pl.BlockSpec(memory_space=pl.ANY)],
        out_specs=vmem,
        compiler_params=pltpu.CompilerParams(vmem_limit_bytes=8 << 20),
        cost_estimate=pl.CostEstimate(
            flops=eigenfunctions.size, bytes_accessed=4 * eigenfunctions.size, transcendentals=0
        ),
    )(grid_count, eigenfunctions, after)


def pair_kernel(x_ref, after_ref, out_ref):
    out_ref[:, :K], out_ref[:, K:] = halves(x_ref[...])


def pair_of(x, after):
    vmem = pl.BlockSpec(memory_space=pltpu.VMEM)
    return pl.pallas_call(
        pair_kernel,
        name="pair",
        out_shape=jax.ShapeDtypeStruct((x.shape[0], 2 * K), BF16),
        in_specs=[vmem, pl.BlockSpec(memory_space=pl.ANY)],
        out_specs=vmem,
        compiler_params=pltpu.CompilerParams(vmem_limit_bytes=4 << 20),
        cost_estimate=pl.CostEstimate(
            flops=4 * x.size, bytes_accessed=8 * x.size, transcendentals=0
        ),
    )(x, after)


def spread_kernel(peers, copies, tiles_ref, after_ref, out_ref):
    size = tiles_ref.shape[0] // peers
    total = tiles_ref[:size]
    for peer in range(1, peers):
        total = total + tiles_ref[peer * size : (peer + 1) * size]
    for copy in range(copies):
        out_ref[copy * size : (copy + 1) * size] = total


def spread(tiles, after, peers, copies):
    vmem = pl.BlockSpec(memory_space=pltpu.VMEM)
    rows, columns = tiles.shape
    return pl.pallas_call(
        lambda *refs: spread_kernel(peers, copies, *refs),
        name="spread",
        out_shape=jax.ShapeDtypeStruct((rows // peers * copies, columns), F32),
        in_specs=[vmem, pl.BlockSpec(memory_space=pl.ANY)],
        out_specs=vmem,
        compiler_params=pltpu.CompilerParams(vmem_limit_bytes=8 << 20),
        cost_estimate=pl.CostEstimate(
            flops=tiles.size, bytes_accessed=12 * tiles.size, transcendentals=0
        ),
    )(tiles, after)


def shards(fields, eigenfunctions, start, grid_count):
    samples = fields.shape[1]
    peers = lax.axis_size("space")
    part = project(fields, eigenfunctions, grid_count, peers)
    length = part.size // peers
    tiles = lax.all_to_all(part.reshape(peers, 1, length), "space", 0, 0, tiled=True)
    masked = mask(grid_count, eigenfunctions, part)
    copies = spread(tiles.reshape(-1, 2 * M), masked, peers, 2 * peers)
    sent = copies.reshape(2 * peers, 1, length)
    mine = lax.all_to_all(sent, ("zh", "space"), 0, 0, tiled=True).reshape(-1, 2 * M)
    first = pair_of(start, copies)
    mine, first = lax.optimization_barrier((mine, first))
    other = lax.ppermute(mine, "core", ((0, 1), (1, 0)))
    return solve(mine, other, first, masked, samples, peers)


def solution(mesh):
    var, space = mesh.devices.shape
    finer = Mesh(mesh.devices.reshape(var // 2, 2, space), ("zh", "core", "space"))
    split = P(("zh", "core"), None, "space")
    return jax.shard_map(
        shards,
        mesh=finer,
        in_specs=(split, split, P(), P()),
        out_specs=(split, P(), P(("zh", "core"), None)),
        check_vma=False,
    )
```

```python
import jax
import jax.numpy as jnp
from jax import lax
from jax.experimental import pallas as pl
from jax.experimental.pallas import tpu as pltpu
from jax.sharding import Mesh, PartitionSpec as P

M = 64
K = 128
SWEEPS = 2
HIGHEST = lax.Precision.HIGHEST
F32 = jnp.float32
BF16 = jnp.bfloat16
STEP = 1024
BLOCK = 32


def dot(left, right, lc, rc, precision=None):
    return lax.dot_general(
        left, right, (((lc,), (rc,)), ((), ())), precision=precision, preferred_element_type=F32
    )


def masked_part(e, first, count):
    columns = first + lax.broadcasted_iota(jnp.int32, e.shape, 1)
    return jnp.where(columns < count, e.astype(F32), 0.0).astype(BF16)


def local_counts(count_ref, points):
    var = lax.axis_index("zh") * lax.axis_size("core") + lax.axis_index("core")
    first = lax.axis_index("space") * points
    return count_ref[2 * var] - first, count_ref[2 * var + 1] - first


def project_kernel(points, peers, count_ref, f_ref, e_ref, out_ref, acc_ref):
    step = pl.program_id(0)
    count0, count1 = local_counts(count_ref, points)
    samples = f_ref.shape[1]
    width = f_ref.shape[2]
    e0 = masked_part(e_ref[0], step * width, count0)
    e1 = masked_part(e_ref[1], step * width, count1)
    none = jnp.zeros_like(e0)
    right0 = jnp.concatenate([e0, none], axis=0)
    right1 = jnp.concatenate([none, e1], axis=0)

    @pl.when(step == 0)
    def _():
        acc_ref[...] = jnp.zeros_like(acc_ref)

    acc_ref[:samples] += dot(f_ref[0], right0, 1, 1) + dot(f_ref[1], right1, 1, 1)
    acc_ref[samples:] += dot(e0, right0, 1, 1) + dot(e1, right1, 1, 1)

    @pl.when(step == pl.num_programs(0) - 1)
    def _():
        own, extra = samples // peers, M // peers
        size = own + extra
        for peer in range(peers):
            out_ref[peer * size : peer * size + own] = acc_ref[peer * own : (peer + 1) * own]
            out_ref[peer * size + own : (peer + 1) * size] = acc_ref[
                samples + peer * extra : samples + (peer + 1) * extra
            ]


def project(fields, eigenfunctions, grid_count, peers):
    _, samples, points = fields.shape
    rows = samples + M
    return pl.pallas_call(
        lambda *refs: project_kernel(points, peers, *refs),
        name="project",
        out_shape=jax.ShapeDtypeStruct((rows, 2 * M), F32),
        grid_spec=pltpu.PrefetchScalarGridSpec(
            num_scalar_prefetch=1,
            grid=(points // STEP,),
            in_specs=[
                pl.BlockSpec((2, samples, STEP), lambda i, c: (0, 0, i)),
                pl.BlockSpec((2, M, STEP), lambda i, c: (0, 0, i)),
            ],
            out_specs=pl.BlockSpec((rows, 2 * M), lambda i, c: (0, 0)),
            scratch_shapes=[pltpu.VMEM((rows, 2 * M), F32)],
        ),
        compiler_params=pltpu.CompilerParams(
            dimension_semantics=("arbitrary",), vmem_limit_bytes=60 << 20
        ),
    )(grid_count, fields, eigenfunctions)


def halves(x):
    high = x.astype(BF16)
    return high, (x - high.astype(F32)).astype(BF16)


def thirds(x):
    high, rest = x.astype(BF16), x
    rest = rest - high.astype(F32)
    middle = rest.astype(BF16)
    return high, middle, (rest - middle.astype(F32)).astype(BF16)


def folded(x):
    half = x.shape[1] // 2
    return x[:, :half] + x[:, half:]


def pair_up(x):
    return jnp.concatenate(halves(x), axis=1)


def product(left, pair):
    return folded(dot(left, jnp.concatenate([pair, pair], axis=0), 1, 0))


def gram_of(image):
    high, middle, low = thirds(image)
    pair = jnp.concatenate([high, middle], axis=1)
    main = folded(
        dot(jnp.concatenate([high, middle], axis=0), jnp.concatenate([pair, pair], axis=0), 0, 0)
    )
    last = dot(high, low, 0, 0)
    return main + (last + last.T)


def times_transposed(image, factor):
    high, middle, low = thirds(image)
    f_high, f_middle, f_low = thirds(factor)
    right = jnp.concatenate(
        [jnp.concatenate([f_high] * 2, axis=1), jnp.concatenate([f_middle] * 2, axis=1)], axis=0
    )
    main = folded(dot(jnp.concatenate([high, middle], axis=1), right, 1, 1))
    return main + dot(
        jnp.concatenate([high, low], axis=1), jnp.concatenate([f_low, f_high], axis=1), 1, 1
    )


def inverse_factor(gram, left_ref, made_ref, out_ref):
    size = gram.shape[0]
    wide = (8, size)
    row = lax.broadcasted_iota(jnp.int32, wide, 0)
    left_ref[...] = gram
    made_ref[...] = jnp.where(
        lax.broadcasted_iota(jnp.int32, (size, size), 0)
        == lax.broadcasted_iota(jnp.int32, (size, size), 1),
        1.0,
        0.0,
    ).astype(F32)
    for first in range(0, size, BLOCK):
        starts = range(first, first + BLOCK, 8)
        left = [left_ref[t : t + 8] for t in starts]
        made = [made_ref[t : t + 8] for t in starts]
        spread = [
            [
                jnp.broadcast_to(x[:, first + j : first + j + 1], wide)
                for j in range(8 * t + 8)
            ]
            for t, x in enumerate(left)
        ]
        scale = [jnp.ones(wide, F32)] * len(left)
        for j in range(BLOCK):
            tile, s = divmod(j, 8)
            root = lax.rsqrt(jnp.broadcast_to(spread[tile][j][s : s + 1], wide))
            scale[tile] = jnp.where(row == s, root, scale[tile])
            inverse = root * root
            factor = {t: spread[t][j] * inverse for t in range(tile, len(left))}
            factor[tile] = jnp.where(row > s, factor[tile], 0.0)
            for other in range(j + 1, BLOCK):
                home, at = divmod(other, 8)
                entry = jnp.broadcast_to(spread[home][j][at : at + 1], wide)
                for t in range(home, len(left)):
                    spread[t][other] = spread[t][other] - factor[t] * entry
            left_row = jnp.broadcast_to(left[tile][s : s + 1], wide)
            made_row = jnp.broadcast_to(made[tile][s : s + 1], wide)
            for t in factor:
                left[t] = left[t] - factor[t] * left_row
                made[t] = made[t] - factor[t] * made_row
        upper = jnp.concatenate([x * y for x, y in zip(left, scale)], axis=0)
        done = jnp.concatenate([x * y for x, y in zip(made, scale)], axis=0)
        out_ref[first : first + BLOCK] = done
        rest = first + BLOCK
        if rest < size:
            a, b, c = thirds(upper[:, rest:])
            d, e, f = thirds(jnp.concatenate([upper, done], axis=1))
            update = dot(
                jnp.concatenate([a, a, b, b, a, c], axis=0),
                jnp.concatenate([d, e, d, e, f, d], axis=0),
                0,
                0,
            )
            left_ref[rest:] = left_ref[rest:] - update[:, :size]
            made_ref[rest:] = made_ref[rest:] - update[:, size:]
    return out_ref[...]


def solve_kernel(
    points, peers, mine_ref, other_ref, start_ref, e_ref,
    load_ref, score_ref, gain_ref,
    high_ref, middle_ref, cov_ref, held_ref, left_ref, made_ref, factor_ref, out_ref, score_out_ref, sem, score_sem,
):
    samples = gain_ref.shape[1]
    joint = start_ref.shape[0]
    own, extra = samples // peers, M // peers
    size = own + extra
    pair = 2 * M
    core, zh = lax.axis_index("core"), lax.axis_index("zh")
    for source, ref in ((core, mine_ref), (1 - core, other_ref)):
        for half in range(2):
            base = half * peers * size
            block = jnp.concatenate(
                [ref[base + p * size : base + p * size + own] for p in range(peers)], axis=0
            )
            mean = jnp.sum(block, axis=0, keepdims=True) / samples
            place = pl.ds(pl.multiple_of((half * 2 + source) * pair, pair), pair)
            high_ref[:, place], middle_ref[:, place] = halves(block - mean)
    high, middle = high_ref[...], middle_ref[...]
    main = dot(high, high, 0, 0)
    cross = dot(high, middle, 0, 0)
    cov = (main + (cross + cross.T)) * (1.0 / (samples - 1))
    cov_ref[:, :joint], cov_ref[:, joint:] = halves(cov)
    basis_pair = start_ref[...]
    for _ in range(SWEEPS):
        image = product(cov_ref[...], basis_pair)
        factor = inverse_factor(gram_of(image), left_ref, made_ref, factor_ref)
        basis = times_transposed(image, factor)
        basis_pair = pair_up(basis)
    held_ref[...] = basis
    first = pl.multiple_of((zh * 2 + core) * pair, pair)
    low = held_ref[pl.ds(first, pair)].astype(BF16)
    copies = []
    for at in range(0, points, STEP):
        for v in range(2):
            e = e_ref[v, :, at : at + STEP]
            out_ref[v, :, at : at + STEP] = dot(low[v * M : (v + 1) * M], e, 0, 0).astype(BF16)
        part = (slice(None), slice(None), slice(at, at + STEP))
        copy = pltpu.make_async_copy(out_ref.at[part], load_ref.at[part], sem.at[at // STEP])
        copy.start()
        copies.append(copy)
    scores = product(jnp.concatenate([high_ref[...], middle_ref[...]], axis=1), basis_pair)
    score_out_ref[...] = scores
    copy = pltpu.make_async_copy(score_out_ref, score_ref, score_sem)
    copy.start()
    copies.append(copy)
    scores_low = scores.astype(BF16)
    base = zh * peers * size
    outer = jnp.concatenate(
        [mine_ref[pl.ds(base + p * size + own, extra)] for p in range(peers)], axis=0
    )
    row = lax.broadcasted_iota(jnp.int32, (pair, pair), 0) // M
    column = lax.broadcasted_iota(jnp.int32, (pair, pair), 1) // M
    outer = jnp.where(row == column, jnp.concatenate([outer, outer], axis=0), 0.0)
    row = lax.broadcasted_iota(jnp.int32, (pair, 2 * K), 0) // M
    column = lax.broadcasted_iota(jnp.int32, (pair, 2 * K), 1) // K
    wide = low.astype(F32)
    blocks = jnp.where(row == column, jnp.concatenate([wide, wide], axis=1), 0.0)
    square = dot(wide, dot(outer, blocks, 1, 0, HIGHEST), 0, 0, HIGHEST)
    square_high, square_middle = halves(-square)
    twice = (2.0 * blocks).astype(BF16)
    place = pl.ds(first, pair)
    along = dot(
        jnp.concatenate(
            [high_ref[:, place], middle_ref[:, place], scores_low, scores_low], axis=1
        ),
        jnp.concatenate([twice, twice, square_high, square_middle], axis=0),
        1,
        0,
    )
    wide_scores = scores_low.astype(F32)
    both_high, both_middle = halves(along * jnp.concatenate([wide_scores, wide_scores], axis=1))
    chosen = lax.broadcasted_iota(jnp.int32, (8, 2 * K), 0)
    chosen = chosen == lax.broadcasted_iota(jnp.int32, (8, 2 * K), 1) // K
    chosen = jnp.where(chosen, 1.0, 0.0).astype(BF16)
    gain = dot(chosen, both_high, 1, 1) + dot(chosen, both_middle, 1, 1)
    gain_ref[...] = gain[:2] / M
    for copy in copies:
        copy.wait()


def solve(mine, other, start, masked, samples, peers):
    points = masked.shape[2]
    joint = start.shape[0]
    vmem = pl.BlockSpec(memory_space=pltpu.VMEM)
    return pl.pallas_call(
        lambda *refs: solve_kernel(points, peers, *refs),
        name="solve",
        out_shape=(
            jax.ShapeDtypeStruct((2, K, points), BF16),
            jax.ShapeDtypeStruct((samples, K), F32),
            jax.ShapeDtypeStruct((2, samples), F32),
        ),
        in_specs=[vmem] * 4,
        out_specs=(pl.BlockSpec(memory_space=pl.ANY), pl.BlockSpec(memory_space=pl.ANY), vmem),
        scratch_shapes=[
            pltpu.VMEM((samples, joint), BF16),
            pltpu.VMEM((samples, joint), BF16),
            pltpu.VMEM((joint, 2 * joint), BF16),
            pltpu.VMEM((joint, K), F32),
            pltpu.VMEM((K, K), F32),
            pltpu.VMEM((K, K), F32),
            pltpu.VMEM((K, K), F32),
            pltpu.VMEM((2, K, points), BF16),
            pltpu.VMEM((samples, K), F32),
            pltpu.SemaphoreType.DMA((points // STEP,)),
            pltpu.SemaphoreType.DMA,
        ],
        compiler_params=pltpu.CompilerParams(vmem_limit_bytes=40 << 20),
    )(mine, other, start, masked)


def mask_kernel(points, count_ref, e_ref, after_ref, out_ref):
    counts = local_counts(count_ref, points)
    for v in range(2):
        out_ref[v] = masked_part(e_ref[v], 0, counts[v])


def mask(grid_count, eigenfunctions, after):
    vmem = pl.BlockSpec(memory_space=pltpu.VMEM)
    points = eigenfunctions.shape[2]
    return pl.pallas_call(
        lambda *refs: mask_kernel(points, *refs),
        name="mask",
        out_shape=jax.ShapeDtypeStruct(eigenfunctions.shape, BF16),
        in_specs=[pl.BlockSpec(memory_space=pltpu.SMEM), vmem, pl.BlockSpec(memory_space=pl.ANY)],
        out_specs=vmem,
        compiler_params=pltpu.CompilerParams(vmem_limit_bytes=8 << 20),
        cost_estimate=pl.CostEstimate(
            flops=eigenfunctions.size, bytes_accessed=4 * eigenfunctions.size, transcendentals=0
        ),
    )(grid_count, eigenfunctions, after)


def pair_kernel(x_ref, after_ref, out_ref):
    out_ref[:, :K], out_ref[:, K:] = halves(x_ref[...])


def pair_of(x, after):
    vmem = pl.BlockSpec(memory_space=pltpu.VMEM)
    return pl.pallas_call(
        pair_kernel,
        name="pair",
        out_shape=jax.ShapeDtypeStruct((x.shape[0], 2 * K), BF16),
        in_specs=[vmem, pl.BlockSpec(memory_space=pl.ANY)],
        out_specs=vmem,
        compiler_params=pltpu.CompilerParams(vmem_limit_bytes=4 << 20),
        cost_estimate=pl.CostEstimate(
            flops=4 * x.size, bytes_accessed=8 * x.size, transcendentals=0
        ),
    )(x, after)


def shards(fields, eigenfunctions, start, grid_count):
    samples = fields.shape[1]
    peers = lax.axis_size("space")
    part = project(fields, eigenfunctions, grid_count, peers)
    length = part.size // peers
    tiles = lax.all_to_all(part.reshape(peers, 1, length), "space", 0, 0, tiled=True)
    masked = mask(grid_count, eigenfunctions, part)
    tile = jnp.sum(tiles, axis=0)
    copies = jnp.broadcast_to(tile, (2 * peers, 1, length))
    mine = lax.all_to_all(copies, ("zh", "space"), 0, 0, tiled=True).reshape(-1, 2 * M)
    first = pair_of(start, tile)
    other = lax.ppermute(mine, "core", ((0, 1), (1, 0)))
    return solve(mine, other, first, masked, samples, peers)


def solution(mesh):
    var, space = mesh.devices.shape
    finer = Mesh(mesh.devices.reshape(var // 2, 2, space), ("zh", "core", "space"))
    split = P(("zh", "core"), None, "space")
    return jax.shard_map(
        shards,
        mesh=finer,
        in_specs=(split, split, P(), P()),
        out_specs=(split, P(), P(("zh", "core"), None)),
        check_vma=False,
    )
```

```python
import jax
import jax.numpy as jnp
from jax import lax
from jax.experimental import pallas as pl
from jax.experimental.pallas import tpu as pltpu
from jax.sharding import Mesh, PartitionSpec as P

M = 64
K = 128
SWEEPS = 2
HIGHEST = lax.Precision.HIGHEST
F32 = jnp.float32
BF16 = jnp.bfloat16
STEP = 1024
BLOCK = 32


def dot(left, right, lc, rc, precision=None):
    return lax.dot_general(
        left, right, (((lc,), (rc,)), ((), ())), precision=precision, preferred_element_type=F32
    )


def masked_part(e, first, count):
    columns = first + lax.broadcasted_iota(jnp.int32, e.shape, 1)
    return jnp.where(columns < count, e.astype(F32), 0.0).astype(BF16)


def local_counts(count_ref, points):
    var = lax.axis_index("zh") * lax.axis_size("core") + lax.axis_index("core")
    first = lax.axis_index("space") * points
    return count_ref[2 * var] - first, count_ref[2 * var + 1] - first


def project_kernel(points, peers, count_ref, f_ref, e_ref, out_ref, acc_ref):
    step = pl.program_id(0)
    count0, count1 = local_counts(count_ref, points)
    samples = f_ref.shape[1]
    width = f_ref.shape[2]
    e0 = masked_part(e_ref[0], step * width, count0)
    e1 = masked_part(e_ref[1], step * width, count1)
    none = jnp.zeros_like(e0)
    right0 = jnp.concatenate([e0, none], axis=0)
    right1 = jnp.concatenate([none, e1], axis=0)

    @pl.when(step == 0)
    def _():
        acc_ref[...] = jnp.zeros_like(acc_ref)

    acc_ref[:samples] += dot(f_ref[0], right0, 1, 1) + dot(f_ref[1], right1, 1, 1)
    acc_ref[samples:] += dot(e0, right0, 1, 1) + dot(e1, right1, 1, 1)

    @pl.when(step == pl.num_programs(0) - 1)
    def _():
        own, extra = samples // peers, M // peers
        size = own + extra
        for peer in range(peers):
            out_ref[peer * size : peer * size + own] = acc_ref[peer * own : (peer + 1) * own]
            out_ref[peer * size + own : (peer + 1) * size] = acc_ref[
                samples + peer * extra : samples + (peer + 1) * extra
            ]


def project(fields, eigenfunctions, grid_count, peers):
    _, samples, points = fields.shape
    rows = samples + M
    return pl.pallas_call(
        lambda *refs: project_kernel(points, peers, *refs),
        name="project",
        out_shape=jax.ShapeDtypeStruct((rows, 2 * M), F32),
        grid_spec=pltpu.PrefetchScalarGridSpec(
            num_scalar_prefetch=1,
            grid=(points // STEP,),
            in_specs=[
                pl.BlockSpec((2, samples, STEP), lambda i, c: (0, 0, i)),
                pl.BlockSpec((2, M, STEP), lambda i, c: (0, 0, i)),
            ],
            out_specs=pl.BlockSpec((rows, 2 * M), lambda i, c: (0, 0)),
            scratch_shapes=[pltpu.VMEM((rows, 2 * M), F32)],
        ),
        compiler_params=pltpu.CompilerParams(
            dimension_semantics=("arbitrary",), vmem_limit_bytes=60 << 20
        ),
    )(grid_count, fields, eigenfunctions)


def halves(x):
    high = x.astype(BF16)
    return high, (x - high.astype(F32)).astype(BF16)


def thirds(x):
    high, rest = x.astype(BF16), x
    rest = rest - high.astype(F32)
    middle = rest.astype(BF16)
    return high, middle, (rest - middle.astype(F32)).astype(BF16)


def folded(x):
    half = x.shape[1] // 2
    return x[:, :half] + x[:, half:]


def pair_up(x):
    return jnp.concatenate(halves(x), axis=1)


def product(high, middle, pair):
    return folded(dot(high, pair, 1, 0)) + dot(middle, pair[:, :K], 1, 0)


def gram_of(image):
    high, middle, low = thirds(image)
    pair = jnp.concatenate([high, middle], axis=1)
    main = folded(
        dot(jnp.concatenate([high, middle], axis=0), jnp.concatenate([pair, pair], axis=0), 0, 0)
    )
    last = dot(high, low, 0, 0)
    return main + (last + last.T)


def times_transposed(image, factor):
    high, middle, low = thirds(image)
    f_high, f_middle, f_low = thirds(factor)
    right = jnp.concatenate(
        [jnp.concatenate([f_high] * 2, axis=1), jnp.concatenate([f_middle] * 2, axis=1)], axis=0
    )
    main = folded(dot(jnp.concatenate([high, middle], axis=1), right, 1, 1))
    return main + dot(
        jnp.concatenate([high, low], axis=1), jnp.concatenate([f_low, f_high], axis=1), 1, 1
    )


def inverse_factor(gram, left_ref, made_ref, out_ref):
    size = gram.shape[0]
    wide = (8, size)
    row = lax.broadcasted_iota(jnp.int32, wide, 0)
    left_ref[...] = gram
    made_ref[...] = jnp.where(
        lax.broadcasted_iota(jnp.int32, (size, size), 0)
        == lax.broadcasted_iota(jnp.int32, (size, size), 1),
        1.0,
        0.0,
    ).astype(F32)
    for first in range(0, size, BLOCK):
        starts = range(first, first + BLOCK, 8)
        left = [left_ref[t : t + 8] for t in starts]
        made = [made_ref[t : t + 8] for t in starts]
        spread = [
            [
                jnp.broadcast_to(x[:, first + j : first + j + 1], wide)
                for j in range(8 * t + 8)
            ]
            for t, x in enumerate(left)
        ]
        scale = [jnp.ones(wide, F32)] * len(left)
        for j in range(BLOCK):
            tile, s = divmod(j, 8)
            root = lax.rsqrt(jnp.broadcast_to(spread[tile][j][s : s + 1], wide))
            scale[tile] = jnp.where(row == s, root, scale[tile])
            inverse = root * root
            factor = {t: spread[t][j] * inverse for t in range(tile, len(left))}
            factor[tile] = jnp.where(row > s, factor[tile], 0.0)
            for other in range(j + 1, BLOCK):
                home, at = divmod(other, 8)
                entry = jnp.broadcast_to(spread[home][j][at : at + 1], wide)
                for t in range(home, len(left)):
                    spread[t][other] = spread[t][other] - factor[t] * entry
            left_row = jnp.broadcast_to(left[tile][s : s + 1], wide)
            made_row = jnp.broadcast_to(made[tile][s : s + 1], wide)
            for t in factor:
                left[t] = left[t] - factor[t] * left_row
                made[t] = made[t] - factor[t] * made_row
        upper = jnp.concatenate([x * y for x, y in zip(left, scale)], axis=0)
        done = jnp.concatenate([x * y for x, y in zip(made, scale)], axis=0)
        out_ref[first : first + BLOCK] = done
        rest = first + BLOCK
        if rest < size:
            a, b, c = thirds(upper[:, rest:])
            d, e, f = thirds(jnp.concatenate([upper, done], axis=1))
            update = dot(
                jnp.concatenate([a, a, b, b, a, c], axis=0),
                jnp.concatenate([d, e, d, e, f, d], axis=0),
                0,
                0,
            )
            left_ref[rest:] = left_ref[rest:] - update[:, :size]
            made_ref[rest:] = made_ref[rest:] - update[:, size:]
    return out_ref[...]


def solve_kernel(
    points, peers, mine_ref, other_ref, start_ref, e_ref,
    load_ref, score_ref, gain_ref,
    high_ref, middle_ref, cov_ref, held_ref, left_ref, made_ref, factor_ref, out_ref, score_out_ref, sem, score_sem,
):
    samples = gain_ref.shape[1]
    joint = start_ref.shape[0]
    own, extra = samples // peers, M // peers
    size = own + extra
    pair = 2 * M
    core, zh = lax.axis_index("core"), lax.axis_index("zh")
    for source, ref in ((core, mine_ref), (1 - core, other_ref)):
        for half in range(2):
            base = half * peers * size
            block = jnp.concatenate(
                [ref[base + p * size : base + p * size + own] for p in range(peers)], axis=0
            )
            mean = jnp.sum(block, axis=0, keepdims=True) / samples
            place = pl.ds(pl.multiple_of((half * 2 + source) * pair, pair), pair)
            high_ref[:, place], middle_ref[:, place] = halves(block - mean)
    high, middle = high_ref[...], middle_ref[...]
    main = dot(high, high, 0, 0)
    cross = dot(high, middle, 0, 0)
    cov = (main + (cross + cross.T)) * (1.0 / (samples - 1))
    cov_ref[:, :joint], cov_ref[:, joint:] = halves(cov)
    basis_pair = start_ref[...]
    for _ in range(SWEEPS):
        image = product(cov_ref[:, :joint], cov_ref[:, joint:], basis_pair)
        factor = inverse_factor(gram_of(image), left_ref, made_ref, factor_ref)
        basis = times_transposed(image, factor)
        basis_pair = pair_up(basis)
    held_ref[...] = basis
    first = pl.multiple_of((zh * 2 + core) * pair, pair)
    low = held_ref[pl.ds(first, pair)].astype(BF16)
    copies = []
    for at in range(0, points, STEP):
        for v in range(2):
            e = e_ref[v, :, at : at + STEP]
            out_ref[v, :, at : at + STEP] = dot(low[v * M : (v + 1) * M], e, 0, 0).astype(BF16)
        part = (slice(None), slice(None), slice(at, at + STEP))
        copy = pltpu.make_async_copy(out_ref.at[part], load_ref.at[part], sem.at[at // STEP])
        copy.start()
        copies.append(copy)
    scores = product(high_ref[...], middle_ref[...], basis_pair)
    score_out_ref[...] = scores
    copy = pltpu.make_async_copy(score_out_ref, score_ref, score_sem)
    copy.start()
    copies.append(copy)
    scores_low = scores.astype(BF16)
    base = zh * peers * size
    outer = jnp.concatenate(
        [mine_ref[pl.ds(base + p * size + own, extra)] for p in range(peers)], axis=0
    )
    row = lax.broadcasted_iota(jnp.int32, (pair, pair), 0) // M
    column = lax.broadcasted_iota(jnp.int32, (pair, pair), 1) // M
    outer = jnp.where(row == column, jnp.concatenate([outer, outer], axis=0), 0.0)
    row = lax.broadcasted_iota(jnp.int32, (pair, 2 * K), 0) // M
    column = lax.broadcasted_iota(jnp.int32, (pair, 2 * K), 1) // K
    wide = low.astype(F32)
    blocks = jnp.where(row == column, jnp.concatenate([wide, wide], axis=1), 0.0)
    square = dot(wide, dot(outer, blocks, 1, 0, HIGHEST), 0, 0, HIGHEST)
    square_high, square_middle = halves(-square)
    twice = (2.0 * blocks).astype(BF16)
    place = pl.ds(first, pair)
    along = dot(
        jnp.concatenate(
            [high_ref[:, place], middle_ref[:, place], scores_low, scores_low], axis=1
        ),
        jnp.concatenate([twice, twice, square_high, square_middle], axis=0),
        1,
        0,
    )
    wide_scores = scores_low.astype(F32)
    both_high, both_middle = halves(along * jnp.concatenate([wide_scores, wide_scores], axis=1))
    chosen = lax.broadcasted_iota(jnp.int32, (8, 2 * K), 0)
    chosen = chosen == lax.broadcasted_iota(jnp.int32, (8, 2 * K), 1) // K
    chosen = jnp.where(chosen, 1.0, 0.0).astype(BF16)
    gain = dot(chosen, both_high, 1, 1) + dot(chosen, both_middle, 1, 1)
    gain_ref[...] = gain[:2] / M
    for copy in copies:
        copy.wait()


def solve(mine, other, start, masked, samples, peers):
    points = masked.shape[2]
    joint = start.shape[0]
    vmem = pl.BlockSpec(memory_space=pltpu.VMEM)
    return pl.pallas_call(
        lambda *refs: solve_kernel(points, peers, *refs),
        name="solve",
        out_shape=(
            jax.ShapeDtypeStruct((2, K, points), BF16),
            jax.ShapeDtypeStruct((samples, K), F32),
            jax.ShapeDtypeStruct((2, samples), F32),
        ),
        in_specs=[vmem] * 4,
        out_specs=(pl.BlockSpec(memory_space=pl.ANY), pl.BlockSpec(memory_space=pl.ANY), vmem),
        scratch_shapes=[
            pltpu.VMEM((samples, joint), BF16),
            pltpu.VMEM((samples, joint), BF16),
            pltpu.VMEM((joint, 2 * joint), BF16),
            pltpu.VMEM((joint, K), F32),
            pltpu.VMEM((K, K), F32),
            pltpu.VMEM((K, K), F32),
            pltpu.VMEM((K, K), F32),
            pltpu.VMEM((2, K, points), BF16),
            pltpu.VMEM((samples, K), F32),
            pltpu.SemaphoreType.DMA((points // STEP,)),
            pltpu.SemaphoreType.DMA,
        ],
        compiler_params=pltpu.CompilerParams(vmem_limit_bytes=40 << 20),
    )(mine, other, start, masked)


def mask_kernel(points, count_ref, e_ref, after_ref, out_ref):
    counts = local_counts(count_ref, points)
    for v in range(2):
        out_ref[v] = masked_part(e_ref[v], 0, counts[v])


def mask(grid_count, eigenfunctions, after):
    vmem = pl.BlockSpec(memory_space=pltpu.VMEM)
    points = eigenfunctions.shape[2]
    return pl.pallas_call(
        lambda *refs: mask_kernel(points, *refs),
        name="mask",
        out_shape=jax.ShapeDtypeStruct(eigenfunctions.shape, BF16),
        in_specs=[pl.BlockSpec(memory_space=pltpu.SMEM), vmem, pl.BlockSpec(memory_space=pl.ANY)],
        out_specs=vmem,
        compiler_params=pltpu.CompilerParams(vmem_limit_bytes=8 << 20),
        cost_estimate=pl.CostEstimate(
            flops=eigenfunctions.size, bytes_accessed=4 * eigenfunctions.size, transcendentals=0
        ),
    )(grid_count, eigenfunctions, after)


def pair_kernel(x_ref, after_ref, out_ref):
    out_ref[:, :K], out_ref[:, K:] = halves(x_ref[...])


def pair_of(x, after):
    vmem = pl.BlockSpec(memory_space=pltpu.VMEM)
    return pl.pallas_call(
        pair_kernel,
        name="pair",
        out_shape=jax.ShapeDtypeStruct((x.shape[0], 2 * K), BF16),
        in_specs=[vmem, pl.BlockSpec(memory_space=pl.ANY)],
        out_specs=vmem,
        compiler_params=pltpu.CompilerParams(vmem_limit_bytes=4 << 20),
        cost_estimate=pl.CostEstimate(
            flops=4 * x.size, bytes_accessed=8 * x.size, transcendentals=0
        ),
    )(x, after)


def shards(fields, eigenfunctions, start, grid_count):
    samples = fields.shape[1]
    peers = lax.axis_size("space")
    part = project(fields, eigenfunctions, grid_count, peers)
    length = part.size // peers
    tiles = lax.all_to_all(part.reshape(peers, 1, length), "space", 0, 0, tiled=True)
    masked = mask(grid_count, eigenfunctions, part)
    tile = jnp.sum(tiles, axis=0)
    copies = jnp.broadcast_to(tile, (2 * peers, 1, length))
    mine = lax.all_to_all(copies, ("zh", "space"), 0, 0, tiled=True).reshape(-1, 2 * M)
    first = pair_of(start, tile)
    other = lax.ppermute(mine, "core", ((0, 1), (1, 0)))
    return solve(mine, other, first, masked, samples, peers)


def solution(mesh):
    var, space = mesh.devices.shape
    finer = Mesh(mesh.devices.reshape(var // 2, 2, space), ("zh", "core", "space"))
    split = P(("zh", "core"), None, "space")
    return jax.shard_map(
        shards,
        mesh=finer,
        in_specs=(split, split, P(), P()),
        out_specs=(split, P(), P(("zh", "core"), None)),
        check_vma=False,
    )
```

```python
import jax
import jax.numpy as jnp
from jax import lax
from jax.experimental import pallas as pl
from jax.experimental.pallas import tpu as pltpu
from jax.sharding import Mesh, PartitionSpec as P

M = 64
K = 128
SWEEPS = 2
HIGHEST = lax.Precision.HIGHEST
F32 = jnp.float32
BF16 = jnp.bfloat16
STEP = 1024
BLOCK = 32


def dot(left, right, lc, rc, precision=None):
    return lax.dot_general(
        left, right, (((lc,), (rc,)), ((), ())), precision=precision, preferred_element_type=F32
    )


def masked_part(e, first, count):
    columns = first + lax.broadcasted_iota(jnp.int32, e.shape, 1)
    return jnp.where(columns < count, e.astype(F32), 0.0).astype(BF16)


def local_counts(count_ref, points):
    var = lax.axis_index("zh") * lax.axis_size("core") + lax.axis_index("core")
    first = lax.axis_index("space") * points
    return count_ref[2 * var] - first, count_ref[2 * var + 1] - first


def project_kernel(points, peers, count_ref, f_ref, e_ref, out_ref, acc_ref):
    step = pl.program_id(0)
    count0, count1 = local_counts(count_ref, points)
    samples = f_ref.shape[1]
    width = f_ref.shape[2]
    e0 = masked_part(e_ref[0], step * width, count0)
    e1 = masked_part(e_ref[1], step * width, count1)
    none = jnp.zeros_like(e0)
    right0 = jnp.concatenate([e0, none], axis=0)
    right1 = jnp.concatenate([none, e1], axis=0)

    @pl.when(step == 0)
    def _():
        acc_ref[...] = jnp.zeros_like(acc_ref)

    acc_ref[:samples] += dot(f_ref[0], right0, 1, 1) + dot(f_ref[1], right1, 1, 1)
    acc_ref[samples:] += dot(e0, right0, 1, 1) + dot(e1, right1, 1, 1)

    @pl.when(step == pl.num_programs(0) - 1)
    def _():
        own, extra = samples // peers, M // peers
        size = own + extra
        for peer in range(peers):
            out_ref[peer * size : peer * size + own] = acc_ref[peer * own : (peer + 1) * own]
            out_ref[peer * size + own : (peer + 1) * size] = acc_ref[
                samples + peer * extra : samples + (peer + 1) * extra
            ]


def project(fields, eigenfunctions, grid_count, peers):
    _, samples, points = fields.shape
    rows = samples + M
    return pl.pallas_call(
        lambda *refs: project_kernel(points, peers, *refs),
        name="project",
        out_shape=jax.ShapeDtypeStruct((rows, 2 * M), F32),
        grid_spec=pltpu.PrefetchScalarGridSpec(
            num_scalar_prefetch=1,
            grid=(points // STEP,),
            in_specs=[
                pl.BlockSpec((2, samples, STEP), lambda i, c: (0, 0, i)),
                pl.BlockSpec((2, M, STEP), lambda i, c: (0, 0, i)),
            ],
            out_specs=pl.BlockSpec((rows, 2 * M), lambda i, c: (0, 0)),
            scratch_shapes=[pltpu.VMEM((rows, 2 * M), F32)],
        ),
        compiler_params=pltpu.CompilerParams(
            dimension_semantics=("arbitrary",), vmem_limit_bytes=60 << 20
        ),
    )(grid_count, fields, eigenfunctions)


def halves(x):
    high = x.astype(BF16)
    return high, (x - high.astype(F32)).astype(BF16)


def thirds(x):
    high, rest = x.astype(BF16), x
    rest = rest - high.astype(F32)
    middle = rest.astype(BF16)
    return high, middle, (rest - middle.astype(F32)).astype(BF16)


def folded(x):
    half = x.shape[1] // 2
    return x[:, :half] + x[:, half:]


def pair_up(x):
    return jnp.concatenate(halves(x), axis=1)


def product(high, middle, pair):
    return folded(dot(high, pair, 1, 0)) + dot(middle, pair[:, :K], 1, 0)


def gram_of(image):
    high, middle, low = thirds(image)
    main = dot(high, high, 0, 0) + dot(middle, middle, 0, 0)
    last = folded(dot(high, jnp.concatenate([middle, low], axis=1), 0, 0))
    return main + (last + last.T)


def times_transposed(image, factor):
    high, middle, low = thirds(image)
    f_high, f_middle, f_low = thirds(factor)
    right = jnp.concatenate(
        [jnp.concatenate([f_high] * 2, axis=1), jnp.concatenate([f_middle] * 2, axis=1)], axis=0
    )
    main = folded(dot(jnp.concatenate([high, middle], axis=1), right, 1, 1))
    return main + dot(
        jnp.concatenate([high, low], axis=1), jnp.concatenate([f_low, f_high], axis=1), 1, 1
    )


def inverse_factor(gram, left_ref, made_ref, out_ref):
    size = gram.shape[0]
    wide = (8, size)
    row = lax.broadcasted_iota(jnp.int32, wide, 0)
    left_ref[...] = gram
    made_ref[...] = jnp.where(
        lax.broadcasted_iota(jnp.int32, (size, size), 0)
        == lax.broadcasted_iota(jnp.int32, (size, size), 1),
        1.0,
        0.0,
    ).astype(F32)
    for first in range(0, size, BLOCK):
        starts = range(first, first + BLOCK, 8)
        left = [left_ref[t : t + 8] for t in starts]
        made = [made_ref[t : t + 8] for t in starts]
        spread = [
            [
                jnp.broadcast_to(x[:, first + j : first + j + 1], wide)
                for j in range(8 * t + 8)
            ]
            for t, x in enumerate(left)
        ]
        scale = [jnp.ones(wide, F32)] * len(left)
        for j in range(BLOCK):
            tile, s = divmod(j, 8)
            root = lax.rsqrt(jnp.broadcast_to(spread[tile][j][s : s + 1], wide))
            scale[tile] = jnp.where(row == s, root, scale[tile])
            inverse = root * root
            factor = {t: spread[t][j] * inverse for t in range(tile, len(left))}
            factor[tile] = jnp.where(row > s, factor[tile], 0.0)
            for other in range(j + 1, BLOCK):
                home, at = divmod(other, 8)
                entry = jnp.broadcast_to(spread[home][j][at : at + 1], wide)
                for t in range(home, len(left)):
                    spread[t][other] = spread[t][other] - factor[t] * entry
            left_row = jnp.broadcast_to(left[tile][s : s + 1], wide)
            made_row = jnp.broadcast_to(made[tile][s : s + 1], wide)
            for t in factor:
                left[t] = left[t] - factor[t] * left_row
                made[t] = made[t] - factor[t] * made_row
        upper = jnp.concatenate([x * y for x, y in zip(left, scale)], axis=0)
        done = jnp.concatenate([x * y for x, y in zip(made, scale)], axis=0)
        out_ref[first : first + BLOCK] = done
        rest = first + BLOCK
        if rest < size:
            a, b, c = thirds(upper[:, rest:])
            d, e, f = thirds(jnp.concatenate([upper, done], axis=1))
            update = dot(
                jnp.concatenate([a, a, b, b, a, c], axis=0),
                jnp.concatenate([d, e, d, e, f, d], axis=0),
                0,
                0,
            )
            left_ref[rest:] = left_ref[rest:] - update[:, :size]
            made_ref[rest:] = made_ref[rest:] - update[:, size:]
    return out_ref[...]


def solve_kernel(
    points, peers, mine_ref, other_ref, start_ref, e_ref,
    load_ref, score_ref, gain_ref,
    high_ref, middle_ref, cov_ref, held_ref, left_ref, made_ref, factor_ref, out_ref, score_out_ref, sem, score_sem,
):
    samples = gain_ref.shape[1]
    joint = start_ref.shape[0]
    own, extra = samples // peers, M // peers
    size = own + extra
    pair = 2 * M
    core, zh = lax.axis_index("core"), lax.axis_index("zh")
    for source, ref in ((core, mine_ref), (1 - core, other_ref)):
        for half in range(2):
            base = half * peers * size
            block = jnp.concatenate(
                [ref[base + p * size : base + p * size + own] for p in range(peers)], axis=0
            )
            mean = jnp.sum(block, axis=0, keepdims=True) / samples
            place = pl.ds(pl.multiple_of((half * 2 + source) * pair, pair), pair)
            high_ref[:, place], middle_ref[:, place] = halves(block - mean)
    high, middle = high_ref[...], middle_ref[...]
    main = dot(high, high, 0, 0)
    cross = dot(high, middle, 0, 0)
    cov = (main + (cross + cross.T)) * (1.0 / (samples - 1))
    cov_ref[:, :joint], cov_ref[:, joint:] = halves(cov)
    basis_pair = start_ref[...]
    for _ in range(SWEEPS):
        image = product(cov_ref[:, :joint], cov_ref[:, joint:], basis_pair)
        factor = inverse_factor(gram_of(image), left_ref, made_ref, factor_ref)
        basis = times_transposed(image, factor)
        basis_pair = pair_up(basis)
    held_ref[...] = basis
    first = pl.multiple_of((zh * 2 + core) * pair, pair)
    low = held_ref[pl.ds(first, pair)].astype(BF16)
    copies = []
    for at in range(0, points, STEP):
        for v in range(2):
            e = e_ref[v, :, at : at + STEP]
            out_ref[v, :, at : at + STEP] = dot(low[v * M : (v + 1) * M], e, 0, 0).astype(BF16)
        part = (slice(None), slice(None), slice(at, at + STEP))
        copy = pltpu.make_async_copy(out_ref.at[part], load_ref.at[part], sem.at[at // STEP])
        copy.start()
        copies.append(copy)
    scores = product(high_ref[...], middle_ref[...], basis_pair)
    score_out_ref[...] = scores
    copy = pltpu.make_async_copy(score_out_ref, score_ref, score_sem)
    copy.start()
    copies.append(copy)
    scores_low = scores.astype(BF16)
    base = zh * peers * size
    outer = jnp.concatenate(
        [mine_ref[pl.ds(base + p * size + own, extra)] for p in range(peers)], axis=0
    )
    row = lax.broadcasted_iota(jnp.int32, (pair, pair), 0) // M
    column = lax.broadcasted_iota(jnp.int32, (pair, pair), 1) // M
    outer = jnp.where(row == column, jnp.concatenate([outer, outer], axis=0), 0.0)
    row = lax.broadcasted_iota(jnp.int32, (pair, 2 * K), 0) // M
    column = lax.broadcasted_iota(jnp.int32, (pair, 2 * K), 1) // K
    wide = low.astype(F32)
    blocks = jnp.where(row == column, jnp.concatenate([wide, wide], axis=1), 0.0)
    square = dot(wide, dot(outer, blocks, 1, 0, HIGHEST), 0, 0, HIGHEST)
    square_high, square_middle = halves(-square)
    twice = (2.0 * blocks).astype(BF16)
    place = pl.ds(first, pair)
    along = dot(
        jnp.concatenate(
            [high_ref[:, place], middle_ref[:, place], scores_low, scores_low], axis=1
        ),
        jnp.concatenate([twice, twice, square_high, square_middle], axis=0),
        1,
        0,
    )
    wide_scores = scores_low.astype(F32)
    both_high, both_middle = halves(along * jnp.concatenate([wide_scores, wide_scores], axis=1))
    chosen = lax.broadcasted_iota(jnp.int32, (8, 2 * K), 0)
    chosen = chosen == lax.broadcasted_iota(jnp.int32, (8, 2 * K), 1) // K
    chosen = jnp.where(chosen, 1.0, 0.0).astype(BF16)
    gain = dot(chosen, both_high, 1, 1) + dot(chosen, both_middle, 1, 1)
    gain_ref[...] = gain[:2] / M
    for copy in copies:
        copy.wait()


def solve(mine, other, start, masked, samples, peers):
    points = masked.shape[2]
    joint = start.shape[0]
    vmem = pl.BlockSpec(memory_space=pltpu.VMEM)
    return pl.pallas_call(
        lambda *refs: solve_kernel(points, peers, *refs),
        name="solve",
        out_shape=(
            jax.ShapeDtypeStruct((2, K, points), BF16),
            jax.ShapeDtypeStruct((samples, K), F32),
            jax.ShapeDtypeStruct((2, samples), F32),
        ),
        in_specs=[vmem] * 4,
        out_specs=(pl.BlockSpec(memory_space=pl.ANY), pl.BlockSpec(memory_space=pl.ANY), vmem),
        scratch_shapes=[
            pltpu.VMEM((samples, joint), BF16),
            pltpu.VMEM((samples, joint), BF16),
            pltpu.VMEM((joint, 2 * joint), BF16),
            pltpu.VMEM((joint, K), F32),
            pltpu.VMEM((K, K), F32),
            pltpu.VMEM((K, K), F32),
            pltpu.VMEM((K, K), F32),
            pltpu.VMEM((2, K, points), BF16),
            pltpu.VMEM((samples, K), F32),
            pltpu.SemaphoreType.DMA((points // STEP,)),
            pltpu.SemaphoreType.DMA,
        ],
        compiler_params=pltpu.CompilerParams(vmem_limit_bytes=40 << 20),
    )(mine, other, start, masked)


def mask_kernel(points, count_ref, e_ref, after_ref, out_ref):
    counts = local_counts(count_ref, points)
    for v in range(2):
        out_ref[v] = masked_part(e_ref[v], 0, counts[v])


def mask(grid_count, eigenfunctions, after):
    vmem = pl.BlockSpec(memory_space=pltpu.VMEM)
    points = eigenfunctions.shape[2]
    return pl.pallas_call(
        lambda *refs: mask_kernel(points, *refs),
        name="mask",
        out_shape=jax.ShapeDtypeStruct(eigenfunctions.shape, BF16),
        in_specs=[pl.BlockSpec(memory_space=pltpu.SMEM), vmem, pl.BlockSpec(memory_space=pl.ANY)],
        out_specs=vmem,
        compiler_params=pltpu.CompilerParams(vmem_limit_bytes=8 << 20),
        cost_estimate=pl.CostEstimate(
            flops=eigenfunctions.size, bytes_accessed=4 * eigenfunctions.size, transcendentals=0
        ),
    )(grid_count, eigenfunctions, after)


def pair_kernel(x_ref, after_ref, out_ref):
    out_ref[:, :K], out_ref[:, K:] = halves(x_ref[...])


def pair_of(x, after):
    vmem = pl.BlockSpec(memory_space=pltpu.VMEM)
    return pl.pallas_call(
        pair_kernel,
        name="pair",
        out_shape=jax.ShapeDtypeStruct((x.shape[0], 2 * K), BF16),
        in_specs=[vmem, pl.BlockSpec(memory_space=pl.ANY)],
        out_specs=vmem,
        compiler_params=pltpu.CompilerParams(vmem_limit_bytes=4 << 20),
        cost_estimate=pl.CostEstimate(
            flops=4 * x.size, bytes_accessed=8 * x.size, transcendentals=0
        ),
    )(x, after)


def shards(fields, eigenfunctions, start, grid_count):
    samples = fields.shape[1]
    peers = lax.axis_size("space")
    part = project(fields, eigenfunctions, grid_count, peers)
    length = part.size // peers
    tiles = lax.all_to_all(part.reshape(peers, 1, length), "space", 0, 0, tiled=True)
    masked = mask(grid_count, eigenfunctions, part)
    tile = jnp.sum(tiles, axis=0)
    copies = jnp.broadcast_to(tile, (2 * peers, 1, length))
    mine = lax.all_to_all(copies, ("zh", "space"), 0, 0, tiled=True).reshape(-1, 2 * M)
    first = pair_of(start, tile)
    other = lax.ppermute(mine, "core", ((0, 1), (1, 0)))
    return solve(mine, other, first, masked, samples, peers)


def solution(mesh):
    var, space = mesh.devices.shape
    finer = Mesh(mesh.devices.reshape(var // 2, 2, space), ("zh", "core", "space"))
    split = P(("zh", "core"), None, "space")
    return jax.shard_map(
        shards,
        mesh=finer,
        in_specs=(split, split, P(), P()),
        out_specs=(split, P(), P(("zh", "core"), None)),
        check_vma=False,
    )
```
